256 devices in a mesh: layer: 8 (over y, core), feat: 32 (over z, x).
Axes of the slice: x: 4, y: 4, z: 8, core: 2. Of those that a mesh axis runs over, the one named last changes fastest.
Arguments:
- top_grad: bfloat16 [256, 4608], P('feat'), may hold values from -6 to 6
- decoder: bfloat16 [8, 16384, 4608], P('layer', 'feat'), may hold values from -0.09375 to 0.09375
- encoder: bfloat16 [8, 16384, 4608], P('layer', 'feat'), may hold values from -0.03125 to 0.03125
- activations: bfloat16 [8, 256, 16384], P('layer', None, 'feat'), may hold values from 0.099609375 to 3
- block_ids: int32 [8, 32, 64], P('layer'), may hold values from 0 to 127, all different within a row
- block_counts: int32 [8, 32], P('layer'), may hold values from 1 to 64, 1024 in all within a row
Outputs:
- attribution: bfloat16 [8, 256, 16384], P('layer', None, 'feat')
- grads: float32 [8, 256, 4608], P('layer', 'feat')
The draws below stay inside these ranges and needn't reach their ends.
Inputs may be any that keep to these rules, and one draw needn't show every extreme that they name: `block_ids`: within one row of the last dimension the ids are distinct; every block id appears somewhere. `block_counts`: for each layer the counts sum to 1024, and some tile of each layer has exactly 64.
All inputs are finite; a program needn't handle non-finite values.
Results may differ from the reference program's by a relative error of at most 0.024.
Values may be sent and summed in bfloat16 or wider, within the bound.
A program may use at most 64 MiB of HBM per device.

```python
import math
import jax
import jax.numpy as jnp
import numpy as np
from jax import lax

D = 4608
BLOCK = 128
TOK_DEV = 8
LAYERS = 8
TILES = 32
TOKENS = 256
FEAT_DEV = 512
FEATURES = 16384
BLOCKS = 128
MAXACT = 64


def steps_of(rng, dims, split, least, high):
    def one(dim, blocks):
        steps = jax.random.uniform(jax.random.fold_in(jax.random.fold_in(rng, 6), dim), (blocks,), jnp.float32, least / len(split), high / len(split))
        return jnp.repeat(jnp.exp(steps), dims[dim] // blocks).reshape((-1,) + (1,) * (len(dims) - dim - 1))

    loudness = one(*split[0])
    for cut in split[1:]:
        loudness = loudness * one(*cut)
    return loudness


def picks_of(rng, rows, count, top, lift):
    sequence = jax.random.permutation(jax.random.fold_in(rng, 1), count)
    pull = sequence
    for power in range(3):
        pull = pull * pull // count
    pull = pull * lift // count
    tickets = jax.random.randint(jax.random.fold_in(rng, 2), (rows, count), 0, 4096) + pull
    fixed_rows = jax.random.permutation(jax.random.fold_in(rng, 3), rows)[jnp.arange(count) % rows]
    tickets = jnp.where(jnp.arange(rows)[:, None] == fixed_rows[None, :], 1 << 14, tickets)
    priority = tickets * count + jnp.arange(count)
    return lax.top_k(priority.astype(jnp.int32), top)[1].astype(jnp.int32)


def length_profile(number_of, total, reach, slope):
    loads = [(1 << 20) // math.isqrt(standing ** slope) + 1 for standing in range(2, number_of + 1)]
    surplus, counts = total - reach - (number_of - 1), [1] * (number_of - 1)
    while surplus > 0:
        movable = [i for i in range(number_of - 1) if counts[i] < reach]
        pool, left = sum([loads[i] for i in movable]), surplus
        for i in movable:
            more = min(reach - counts[i], max(1, left * loads[i] // pool), surplus)
            counts[i] = counts[i] + more
            surplus = surplus - more
    return np.array([reach] + counts)


def uneven(stream_key, count, total, limit, skew):
    if count == 2:
        one = jax.random.randint(stream_key, (), max(1, total - limit), min(limit, total - 1) + 1)
        return jnp.stack([one, total - one])
    sizes = jnp.asarray(length_profile(count, total, limit, skew), jnp.int32)
    couples = (count - 1) // 2
    donor, taker = sizes[1:1 + 2 * couples:2], sizes[2:2 + 2 * couples:2]
    margin = jnp.minimum(donor - 1, limit - taker)
    shifted = jax.random.randint(jax.random.fold_in(stream_key, 1), (couples,), 0, 1 << 20) % (margin + 1)
    sizes = sizes.at[1:1 + 2 * couples:2].set(donor - shifted).at[2:2 + 2 * couples:2].set(taker + shifted)
    return sizes[jax.random.permutation(jax.random.fold_in(stream_key, 2), count)]


def bell_draw(own_key, dims, spread, bound, cuts=(), dtype=jnp.bfloat16):
    drawn = spread * jax.random.normal(own_key, dims, jnp.float32)
    if cuts:
        drawn = drawn * steps_of(own_key, dims, cuts, -0.22, 0.18)
    return jnp.clip(drawn, -bound, bound).astype(dtype)


def setup_inputs(seed: int = 0) -> dict:
    keys = jax.random.split(jax.random.key(seed), 7)
    return {
        "top_grad": bell_draw(keys[0], (TOKENS, D), 1.0, 6.0, ((0, 32),)),
        "decoder": bell_draw(keys[1], (LAYERS, FEATURES, D), D ** -0.5, 0.09375, ((0, 8), (1, 32))),
        "encoder": bell_draw(keys[2], (LAYERS, FEATURES, D), (4 * MAXACT * BLOCK) ** -0.5, 0.03125, ((0, 8), (1, 32))),
        "activations": jnp.clip(jnp.exp(math.log(3.0) - 3.4051113 * jax.random.uniform(keys[3], (LAYERS, TOKENS, FEATURES), jnp.float32) ** steps_of(keys[3], (LAYERS, TOKENS, FEATURES), ((0, 8), (2, 32)), -0.2, 0.2)), 0.099609375, 3.0).astype(jnp.bfloat16),
        "block_ids": picks_of(keys[4], LAYERS * TILES, BLOCKS, MAXACT, 8192).reshape((LAYERS, TILES, MAXACT)),
        "block_counts": jax.vmap(lambda own: uneven(own, TILES, TILES * MAXACT // 2, MAXACT, 2))(jax.random.split(keys[5], LAYERS)).reshape((LAYERS, TILES)).astype(jnp.int32),
    }


def reference(top_grad, decoder, encoder, activations, block_ids, block_counts):
    listed = jnp.arange(MAXACT)[None, None, :] < block_counts[:, :, None]
    block_range = jnp.arange(BLOCKS)
    matches = (block_ids[:, :, :, None] == block_range[None, None, None, :]) & listed[:, :, :, None]
    tile_mask = jnp.any(matches, axis=2).astype(jnp.float32)
    gradient = top_grad.astype(jnp.float32)
    attr_list = [None] * LAYERS
    grad_list = [None] * LAYERS
    for layer_index in reversed(range(LAYERS)):
        feature_mask = jnp.repeat(jnp.repeat(tile_mask[layer_index], TOK_DEV, axis=0), BLOCK, axis=1)
        scores = jnp.dot(gradient.astype(jnp.bfloat16), decoder[layer_index].T, preferred_element_type=jnp.float32)
        attributed = (scores * activations[layer_index].astype(jnp.float32) * feature_mask).astype(jnp.bfloat16)
        attr_groups = jnp.transpose(attributed.reshape(TOKENS, TILES, FEAT_DEV), (1, 0, 2))
        enc_groups = encoder[layer_index].reshape(TILES, FEAT_DEV, D)

        def add_group(running, pieces):
            group_term = jnp.dot(pieces[0], pieces[1], preferred_element_type=jnp.float32).astype(jnp.bfloat16)
            group_term = lax.optimization_barrier(group_term)
            return running + group_term.astype(jnp.float32), None

        summed, unused = lax.scan(add_group, jnp.zeros((TOKENS, D), jnp.float32), (attr_groups, enc_groups))
        gradient = gradient + summed
        attr_list[layer_index] = attributed
        grad_list[layer_index] = gradient
    return jnp.stack(attr_list), jnp.stack(grad_list)
```

```python
import functools

import jax
import jax.numpy as jnp
from jax import lax
from jax.experimental import pallas as pl
from jax.experimental.pallas import tpu as pltpu
from jax.sharding import PartitionSpec as P

BLOCK = 128
MESH = pl.DeviceIdType.MESH
NX = 4


def kernel(
    layers, nz, nx, top_ref, dec_hbm, enc_hbm, act_hbm, ids_ref, cnt_ref, attr_out, grad_out,
    dec_v, enc_v, act_v, gate_v, attr_v, hsend, hout, gin, gnew, agbuf, pbuf, pown, rsx, zsend, rsz, coll,
    load_sem, attr_sem, top_send, top_recv, agz_send, agz_recv, agx_send, agx_recv, rsx_send, rsx_recv,
    rsz_send, rsz_recv, gin_send, gin_recv, coll_send, coll_recv,
):
    feats, width = dec_v.shape[1], dec_v.shape[2]
    tok = top_ref.shape[0]
    rows = nz * tok
    groups = nx
    layer = lax.axis_index("layer")
    feat = lax.axis_index("feat")
    z = feat // nx
    x = feat % nx
    lower = (layer + layers - 1) % layers
    upper = (layer + 1) % layers
    is_top = layer == layers - 1

    def z_peer(d):
        return ((z + d) % nz) * nx + x

    def x_peer(d):
        return z * nx + (x + d) % nx

    def cols(j):
        return pl.ds(pl.multiple_of(j * width, 128), width)

    def remote(src, dst, send, recv, where, peer):
        return pltpu.make_async_remote_copy(
            src_ref=src, dst_ref=dst, send_sem=send, recv_sem=recv, device_id=(where, peer), device_id_type=MESH
        )

    def settle(ref, sem):
        pltpu.make_async_copy(ref, ref, sem).wait()

    loads = [pltpu.make_async_copy(act_hbm.at[:, j], act_v.at[j], load_sem.at[2 * nx + j]) for j in range(nx)]
    loads += [pltpu.make_async_copy(dec_hbm.at[:, cols(j)], dec_v.at[j], load_sem.at[j]) for j in range(nx)]
    loads += [pltpu.make_async_copy(enc_hbm.at[:, cols(j)], enc_v.at[j], load_sem.at[nx + j]) for j in range(nx)]
    for load in loads:
        load.start()

    barrier = pltpu.get_barrier_semaphore()
    for d in range(1, nx):
        pl.semaphore_signal(barrier, inc=1, device_id=(layer, x_peer(d)), device_id_type=MESH)
    for d in range(1, nz):
        pl.semaphore_signal(barrier, inc=1, device_id=(layer, z_peer(d)), device_id_type=MESH)
    for d in range(nz):
        pl.semaphore_signal(barrier, inc=1, device_id=(lower, z_peer(d)), device_id_type=MESH)
        pl.semaphore_signal(barrier, inc=1, device_id=(upper, z_peer(d)), device_id_type=MESH)
    pl.semaphore_wait(barrier, nx - 1 + nz - 1 + 2 * nz)

    far_z = sorted(range(1, nz), key=lambda d: -min(d, nz - d))
    far_x = sorted(range(1, nx), key=lambda d: -min(d, nx - d))
    near_x = far_x[::-1]

    @pl.when(is_top)
    def _():
        pltpu.make_async_copy(top_ref.at[:, cols(x)], hsend.at[x], top_recv).start()
        for d in far_x:
            remote(
                top_ref.at[:, cols((x + d) % nx)], hsend.at[x], top_send, top_recv, layer, x_peer(d)
            ).start()
        settle(hsend, top_recv)

        @pl.loop(0, groups)
        def _(g):
            for d in far_z:
                remote(hsend.at[g], agbuf.at[g, x, z], agz_send, agz_recv.at[g], layer, z_peer(d)).start()
            pltpu.make_async_copy(hsend.at[g], agbuf.at[g, x, z], agz_recv.at[g]).start()
            gin[g] = hsend[g].astype(jnp.float32)

    tiles = nz * nx
    listed_ids = ids_ref[...]
    width_ids = listed_ids.shape[1]
    eye = lax.broadcasted_iota(jnp.int32, (tiles, tiles), 0) == lax.broadcasted_iota(jnp.int32, (tiles, tiles), 1)
    counts = jnp.sum(jnp.where(eye, jnp.broadcast_to(cnt_ref[...], (tiles, tiles)), 0), axis=1, keepdims=True)
    listed = lax.broadcasted_iota(jnp.int32, (tiles, width_ids), 1) < counts
    blk_dev = feats // BLOCK
    parts = []
    for b in range(blk_dev):
        hit = jnp.where(listed & (listed_ids == feat * blk_dev + b), 1.0, 0.0)
        parts.append(jnp.broadcast_to(jnp.max(hit, axis=1, keepdims=True), (tiles, BLOCK)))
    tile_mask = jnp.concatenate(parts, axis=1).astype(jnp.bfloat16)
    for j in range(nx):
        loads[j].wait()
    row_tile = (lax.broadcasted_iota(jnp.int32, (rows, tiles), 0) // tok) * nx
    col_tile = lax.broadcasted_iota(jnp.int32, (rows, tiles), 1)
    for j in range(groups):
        pick = jnp.where(row_tile + j == col_tile, 1.0, 0.0).astype(jnp.bfloat16)
        mask = jnp.dot(pick, tile_mask, preferred_element_type=jnp.float32)
        gate_v[j] = act_v[j].astype(jnp.float32).reshape(rows, feats) * mask
    for load in loads[nx:]:
        load.wait()

    def forward(g):
        settle(agbuf.at[g, x], agz_recv.at[g])
        for d in far_x:
            remote(
                agbuf.at[g, x], agbuf.at[g, x], agx_send, agx_recv.at[g, d - 1], layer, x_peer(d)
            ).start()

    def scores_of(g, j):
        h = agbuf[g, j].reshape(rows, width)
        return lax.dot_general(h, dec_v[j], (((1,), (1,)), ((), ())), preferred_element_type=jnp.float32)

    def attribute(g):
        total = scores_of(g, x)
        for d in near_x:
            j = (x + nx - d) % nx
            settle(agbuf.at[g, j], agx_recv.at[g, d - 1])
            total = total + scores_of(g, j)
        attr = total * gate_v[g]
        attr_v[g] = attr.reshape(nz, tok, feats).astype(jnp.bfloat16)
        attr = attr.astype(jnp.bfloat16)
        pltpu.make_async_copy(attr_v.at[g], attr_out.at[:, g], attr_sem).start()
        for d in far_x:
            j = (x + d) % nx
            part = jnp.dot(attr, enc_v[j], preferred_element_type=jnp.float32)
            pbuf[g, d - 1] = part.astype(jnp.bfloat16)
            remote(
                pbuf.at[g, d - 1], rsx.at[g, d - 1], rsx_send, rsx_recv.at[g, d - 1], layer, x_peer(d)
            ).start()
        pown[g] = jnp.dot(attr, enc_v[x], preferred_element_type=jnp.float32)

    def reduce_x(g):
        total = pown[g]
        for d in near_x:
            settle(rsx.at[g, d - 1], rsx_recv.at[g, d - 1])
            total = total + rsx[g, d - 1].astype(jnp.float32)
        zsend[g] = total.reshape(nz, tok, width).astype(jnp.bfloat16)
        for d in far_z:
            remote(
                zsend.at[g, (z + d) % nz], rsz.at[g, d - 1], rsz_send, rsz_recv.at[g], layer, z_peer(d)
            ).start()

    def reduce_z(g):
        @pl.when(jnp.logical_not(is_top))
        def _():
            settle(gin.at[g], gin_recv.at[g])

        settle(rsz.at[g], rsz_recv.at[g])
        total = zsend[g, z].astype(jnp.float32)
        for d in range(1, nz):
            total = total + rsz[g, d - 1].astype(jnp.float32)
        total = total + gin[g]
        gnew[g] = total
        hout[g] = total.astype(jnp.bfloat16)

        @pl.when(layer > 0)
        def _():
            for d in far_z + [0]:
                remote(hout.at[g], agbuf.at[g, x, z], agz_send, agz_recv.at[g], lower, z_peer(d)).start()
            remote(gnew.at[g], gin.at[g], gin_send, gin_recv.at[g], lower, feat).start()

        @pl.when(x != g)
        def _():
            remote(gnew.at[g], coll.at[x], coll_send, coll_recv, layer, z * nx + g).start()

        @pl.when(x == g)
        def _():
            pltpu.make_async_copy(gnew.at[g], coll.at[x], coll_recv).start()

    @pl.loop(0, groups + 1)
    def _(step):
        @pl.when(step < groups)
        def _():
            forward(step)

        @pl.when(step > 0)
        def _():
            reduce_x(step - 1)

        @pl.when(step < groups)
        def _():
            attribute(step)

        @pl.when(step > 0)
        def _():
            reduce_z(step - 1)

    settle(coll, coll_recv)
    for j in range(nx):
        grad_out[:, j * width:(j + 1) * width] = coll[j]

    settle(attr_v, attr_sem)
    settle(agbuf.at[:, pl.ds(0, nx - 1)], agx_send)
    settle(pbuf, rsx_send)
    settle(zsend.at[:, pl.ds(0, nz - 1)], rsz_send)
    settle(coll.at[pl.ds(0, nx - 1)], coll_send)

    @pl.when(is_top)
    def _():
        settle(hsend.at[pl.ds(0, nx - 1)], top_send)
        settle(zsend.at[:, pl.ds(0, nz - 1)], agz_send)

    @pl.when(layer > 0)
    def _():
        settle(zsend, agz_send)
        settle(gnew, gin_send)


def body(nx, top_grad, decoder, encoder, activations, block_ids, block_counts):
    layers = lax.axis_size("layer")
    tiles = lax.axis_size("feat")
    nz = tiles // nx
    dec, enc = decoder[0], encoder[0]
    feats, model = dec.shape
    width = model // nx
    tok = top_grad.shape[0]
    rows = nz * tok
    act = activations[0].reshape(nz, nx, tok, feats)
    bf16, f32 = jnp.bfloat16, jnp.float32
    dma = pltpu.SemaphoreType.DMA
    vmem = pl.BlockSpec(memory_space=pltpu.VMEM)
    hbm = pl.BlockSpec(memory_space=pl.ANY)
    attr, grads = pl.pallas_call(
        functools.partial(kernel, layers, nz, nx),
        out_shape=(
            jax.ShapeDtypeStruct((nz, nx, tok, feats), bf16),
            jax.ShapeDtypeStruct((tok, model), f32),
        ),
        in_specs=[vmem, hbm, hbm, hbm, vmem, vmem],
        out_specs=(hbm, vmem),
        scratch_shapes=[
            pltpu.VMEM((nx, feats, width), bf16),
            pltpu.VMEM((nx, feats, width), bf16),
            pltpu.VMEM((nx, nz, tok, feats), bf16),
            pltpu.VMEM((nx, rows, feats), f32),
            pltpu.VMEM((nx, nz, tok, feats), bf16),
            pltpu.VMEM((nx, tok, width), bf16),
            pltpu.VMEM((nx, tok, width), bf16),
            pltpu.VMEM((nx, tok, width), f32),
            pltpu.VMEM((nx, tok, width), f32),
            pltpu.VMEM((nx, nx, nz, tok, width), bf16),
            pltpu.VMEM((nx, nx - 1, rows, width), bf16),
            pltpu.VMEM((nx, rows, width), f32),
            pltpu.VMEM((nx, nx - 1, rows, width), bf16),
            pltpu.VMEM((nx, nz, tok, width), bf16),
            pltpu.VMEM((nx, nz - 1, tok, width), bf16),
            pltpu.VMEM((nx, tok, width), f32),
            dma((3 * nx,)),
            dma,
            dma,
            dma,
            dma,
            dma((nx,)),
            dma,
            dma((nx, nx - 1)),
            dma,
            dma((nx, nx - 1)),
            dma,
            dma((nx,)),
            dma,
            dma((nx,)),
            dma,
            dma,
        ],
        compiler_params=pltpu.CompilerParams(
            collective_id=0, has_side_effects=True, vmem_limit_bytes=60 * 1024 * 1024
        ),
    )(top_grad, dec, enc, act, block_ids[0], block_counts)
    return (attr.reshape(1, tiles * tok, feats), grads[None])


def solution(mesh, nx=NX):
    placed = (
        P("feat", None),
        P("layer", "feat", None),
        P("layer", "feat", None),
        P("layer", None, "feat"),
        P("layer", None, None),
        P("layer", None),
    )
    return jax.shard_map(
        functools.partial(body, nx),
        mesh=mesh,
        in_specs=placed,
        out_specs=(P("layer", None, "feat"), P("layer", "feat", None)),
        check_vma=False,
    )
```

```python
import functools

import jax
import jax.numpy as jnp
from jax import lax
from jax.experimental import pallas as pl
from jax.experimental.pallas import tpu as pltpu
from jax.sharding import PartitionSpec as P

BLOCK = 128
MESH = pl.DeviceIdType.MESH
NX = 4


def kernel(
    layers, nz, nx, top_ref, dec_hbm, enc_hbm, act_hbm, ids_ref, cnt_ref, attr_out, grad_out,
    dec_v, enc_v, act_v, gate_v, attr_v, hsend, hout, gin, gnew, agbuf, pbuf, pown, rsx, zsend, rsz, coll,
    load_sem, attr_sem, top_send, top_recv, agz_send, agz_recv, agx_send, agx_recv, rsx_send, rsx_recv,
    rsz_send, rsz_recv, gin_send, gin_recv, coll_send, coll_recv,
):
    feats, width = dec_v.shape[1], dec_v.shape[2]
    tok = top_ref.shape[0]
    rows = nz * tok
    groups = nx
    layer = lax.axis_index("layer")
    feat = lax.axis_index("feat")
    z = feat // nx
    x = feat % nx
    lower = (layer + layers - 1) % layers
    upper = (layer + 1) % layers
    is_top = layer == layers - 1

    def z_peer(d):
        return ((z + d) % nz) * nx + x

    def x_peer(d):
        return z * nx + (x + d) % nx

    def cols(j):
        return pl.ds(pl.multiple_of(j * width, 128), width)

    def remote(src, dst, send, recv, where, peer):
        return pltpu.make_async_remote_copy(
            src_ref=src, dst_ref=dst, send_sem=send, recv_sem=recv, device_id=(where, peer), device_id_type=MESH
        )

    def settle(ref, sem):
        pltpu.make_async_copy(ref, ref, sem).wait()

    loads = [pltpu.make_async_copy(act_hbm.at[:, j], act_v.at[j], load_sem.at[2 * nx + j]) for j in range(nx)]
    loads += [pltpu.make_async_copy(dec_hbm.at[:, cols(j)], dec_v.at[j], load_sem.at[j]) for j in range(nx)]
    loads += [pltpu.make_async_copy(enc_hbm.at[:, cols(j)], enc_v.at[j], load_sem.at[nx + j]) for j in range(nx)]
    for load in loads:
        load.start()

    barrier = pltpu.get_barrier_semaphore()
    for d in range(1, nx):
        pl.semaphore_signal(barrier, inc=1, device_id=(layer, x_peer(d)), device_id_type=MESH)
    for d in range(1, nz):
        pl.semaphore_signal(barrier, inc=1, device_id=(layer, z_peer(d)), device_id_type=MESH)
    for d in range(nz):
        pl.semaphore_signal(barrier, inc=1, device_id=(lower, z_peer(d)), device_id_type=MESH)
        pl.semaphore_signal(barrier, inc=1, device_id=(upper, z_peer(d)), device_id_type=MESH)
    pl.semaphore_wait(barrier, nx - 1 + nz - 1 + 2 * nz)

    far_z = sorted(range(1, nz), key=lambda d: -min(d, nz - d))
    far_x = sorted(range(1, nx), key=lambda d: -min(d, nx - d))
    near_x = far_x[::-1]

    @pl.when(is_top)
    def _():
        pltpu.make_async_copy(top_ref.at[:, cols(x)], hsend.at[x], top_recv).start()
        for d in far_x:
            remote(
                top_ref.at[:, cols((x + d) % nx)], hsend.at[x], top_send, top_recv, layer, x_peer(d)
            ).start()
        settle(hsend, top_recv)

        @pl.loop(0, groups)
        def _(g):
            for d in far_z:
                remote(hsend.at[g], agbuf.at[g, x, z], agz_send, agz_recv.at[g, d], layer, z_peer(d)).start()
            pltpu.make_async_copy(hsend.at[g], agbuf.at[g, x, z], agz_recv.at[g, 0]).start()
            gin[g] = hsend[g].astype(jnp.float32)

    tiles = nz * nx
    listed_ids = ids_ref[...]
    width_ids = listed_ids.shape[1]
    eye = lax.broadcasted_iota(jnp.int32, (tiles, tiles), 0) == lax.broadcasted_iota(jnp.int32, (tiles, tiles), 1)
    counts = jnp.sum(jnp.where(eye, jnp.broadcast_to(cnt_ref[...], (tiles, tiles)), 0), axis=1, keepdims=True)
    listed = lax.broadcasted_iota(jnp.int32, (tiles, width_ids), 1) < counts
    blk_dev = feats // BLOCK
    parts = []
    for b in range(blk_dev):
        hit = jnp.where(listed & (listed_ids == feat * blk_dev + b), 1.0, 0.0)
        parts.append(jnp.broadcast_to(jnp.max(hit, axis=1, keepdims=True), (tiles, BLOCK)))
    tile_mask = jnp.concatenate(parts, axis=1).astype(jnp.bfloat16)
    for j in range(nx):
        loads[j].wait()
    row_tile = (lax.broadcasted_iota(jnp.int32, (rows, tiles), 0) // tok) * nx
    col_tile = lax.broadcasted_iota(jnp.int32, (rows, tiles), 1)
    for j in range(groups):
        pick = jnp.where(row_tile + j == col_tile, 1.0, 0.0).astype(jnp.bfloat16)
        mask = jnp.dot(pick, tile_mask, preferred_element_type=jnp.float32)
        gate_v[j] = act_v[j].astype(jnp.float32).reshape(rows, feats) * mask
    for load in loads[nx:]:
        load.wait()

    def forward(g):
        for d in [0] + far_z[::-1]:
            k = (z + nz - d) % nz
            settle(agbuf.at[g, x, k], agz_recv.at[g, d])
            for e in far_x:
                remote(
                    agbuf.at[g, x, k], agbuf.at[g, x, k], agx_send, agx_recv.at[g, e - 1], layer, x_peer(e)
                ).start()

    def scores_of(g, j):
        h = agbuf[g, j].reshape(rows, width)
        return lax.dot_general(h, dec_v[j], (((1,), (1,)), ((), ())), preferred_element_type=jnp.float32)

    def attribute(g):
        total = scores_of(g, x)
        for d in near_x:
            j = (x + nx - d) % nx
            settle(agbuf.at[g, j], agx_recv.at[g, d - 1])
            total = total + scores_of(g, j)
        attr = total * gate_v[g]
        attr_v[g] = attr.reshape(nz, tok, feats).astype(jnp.bfloat16)
        attr = attr.astype(jnp.bfloat16)
        pltpu.make_async_copy(attr_v.at[g], attr_out.at[:, g], attr_sem).start()
        for d in far_x:
            part = jnp.dot(attr, enc_v[(x + d) % nx], preferred_element_type=jnp.float32)
            pbuf[g, d - 1] = part.reshape(nz, tok, width).astype(jnp.bfloat16)
        for d in far_z + [0]:
            k = (z + d) % nz
            for e in far_x:
                remote(
                    pbuf.at[g, e - 1, k], rsx.at[g, e - 1, k], rsx_send, rsx_recv.at[g, d], layer, x_peer(e)
                ).start()
        own = jnp.dot(attr, enc_v[x], preferred_element_type=jnp.float32)
        pown[g] = own.reshape(nz, tok, width)

    def reduce_x(g):
        for d in far_z + [0]:
            k = (z + d) % nz
            settle(rsx.at[g, :, k], rsx_recv.at[g, d])
            total = pown[g, k]
            for e in near_x:
                total = total + rsx[g, e - 1, k].astype(jnp.float32)
            zsend[g, k] = total.astype(jnp.bfloat16)
            if d:
                remote(zsend.at[g, k], rsz.at[g, d - 1], rsz_send, rsz_recv.at[g], layer, z_peer(d)).start()

    def reduce_z(g):
        @pl.when(jnp.logical_not(is_top))
        def _():
            settle(gin.at[g], gin_recv.at[g])

        settle(rsz.at[g], rsz_recv.at[g])
        total = zsend[g, z].astype(jnp.float32)
        for d in range(1, nz):
            total = total + rsz[g, d - 1].astype(jnp.float32)
        total = total + gin[g]
        gnew[g] = total
        hout[g] = total.astype(jnp.bfloat16)

        @pl.when(layer > 0)
        def _():
            for d in far_z + [0]:
                remote(hout.at[g], agbuf.at[g, x, z], agz_send, agz_recv.at[g, d], lower, z_peer(d)).start()
            remote(gnew.at[g], gin.at[g], gin_send, gin_recv.at[g], lower, feat).start()

        @pl.when(x != g)
        def _():
            remote(gnew.at[g], coll.at[x], coll_send, coll_recv, layer, z * nx + g).start()

        @pl.when(x == g)
        def _():
            pltpu.make_async_copy(gnew.at[g], coll.at[x], coll_recv).start()

    @pl.loop(0, groups)
    def _(step):
        forward(step)
        attribute(step)
        reduce_x(step)
        reduce_z(step)

    settle(coll, coll_recv)
    for j in range(nx):
        grad_out[:, j * width:(j + 1) * width] = coll[j]

    settle(attr_v, attr_sem)
    settle(agbuf.at[:, pl.ds(0, nx - 1)], agx_send)
    settle(pbuf, rsx_send)
    settle(zsend.at[:, pl.ds(0, nz - 1)], rsz_send)
    settle(coll.at[pl.ds(0, nx - 1)], coll_send)

    @pl.when(is_top)
    def _():
        settle(hsend.at[pl.ds(0, nx - 1)], top_send)
        settle(zsend.at[:, pl.ds(0, nz - 1)], agz_send)

    @pl.when(layer > 0)
    def _():
        settle(zsend, agz_send)
        settle(gnew, gin_send)


def body(nx, top_grad, decoder, encoder, activations, block_ids, block_counts):
    layers = lax.axis_size("layer")
    tiles = lax.axis_size("feat")
    nz = tiles // nx
    dec, enc = decoder[0], encoder[0]
    feats, model = dec.shape
    width = model // nx
    tok = top_grad.shape[0]
    rows = nz * tok
    act = activations[0].reshape(nz, nx, tok, feats)
    bf16, f32 = jnp.bfloat16, jnp.float32
    dma = pltpu.SemaphoreType.DMA
    vmem = pl.BlockSpec(memory_space=pltpu.VMEM)
    hbm = pl.BlockSpec(memory_space=pl.ANY)
    attr, grads = pl.pallas_call(
        functools.partial(kernel, layers, nz, nx),
        out_shape=(
            jax.ShapeDtypeStruct((nz, nx, tok, feats), bf16),
            jax.ShapeDtypeStruct((tok, model), f32),
        ),
        in_specs=[vmem, hbm, hbm, hbm, vmem, vmem],
        out_specs=(hbm, vmem),
        scratch_shapes=[
            pltpu.VMEM((nx, feats, width), bf16),
            pltpu.VMEM((nx, feats, width), bf16),
            pltpu.VMEM((nx, nz, tok, feats), bf16),
            pltpu.VMEM((nx, rows, feats), f32),
            pltpu.VMEM((nx, nz, tok, feats), bf16),
            pltpu.VMEM((nx, tok, width), bf16),
            pltpu.VMEM((nx, tok, width), bf16),
            pltpu.VMEM((nx, tok, width), f32),
            pltpu.VMEM((nx, tok, width), f32),
            pltpu.VMEM((nx, nx, nz, tok, width), bf16),
            pltpu.VMEM((nx, nx - 1, nz, tok, width), bf16),
            pltpu.VMEM((nx, nz, tok, width), f32),
            pltpu.VMEM((nx, nx - 1, nz, tok, width), bf16),
            pltpu.VMEM((nx, nz, tok, width), bf16),
            pltpu.VMEM((nx, nz - 1, tok, width), bf16),
            pltpu.VMEM((nx, tok, width), f32),
            dma((3 * nx,)),
            dma,
            dma,
            dma,
            dma,
            dma((nx, nz)),
            dma,
            dma((nx, nx - 1)),
            dma,
            dma((nx, nz)),
            dma,
            dma((nx,)),
            dma,
            dma((nx,)),
            dma,
            dma,
        ],
        compiler_params=pltpu.CompilerParams(
            collective_id=0, has_side_effects=True, vmem_limit_bytes=60 * 1024 * 1024
        ),
    )(top_grad, dec, enc, act, block_ids[0], block_counts)
    return (attr.reshape(1, tiles * tok, feats), grads[None])


def solution(mesh, nx=NX):
    placed = (
        P("feat", None),
        P("layer", "feat", None),
        P("layer", "feat", None),
        P("layer", None, "feat"),
        P("layer", None, None),
        P("layer", None),
    )
    return jax.shard_map(
        functools.partial(body, nx),
        mesh=mesh,
        in_specs=placed,
        out_specs=(P("layer", None, "feat"), P("layer", "feat", None)),
        check_vma=False,
    )
```

```python
import functools

import jax
import jax.numpy as jnp
from jax import lax
from jax.experimental import pallas as pl
from jax.experimental.pallas import tpu as pltpu
from jax.sharding import PartitionSpec as P

BLOCK = 128
MESH = pl.DeviceIdType.MESH
NX = 4
NEAR_IN = 2
NEAR_OUT = 2


def side_columns(nz, reach):
    near = [d for d in sorted(range(nz), key=lambda d: min(d, nz - d)) if min(d, nz - d) <= reach]
    return {d: 1 - 2 * (i % 2) for i, d in enumerate(near)}


def kernel(
    layers, nz, nx, top_ref, dec_hbm, enc_hbm, act_hbm, ids_ref, cnt_ref, attr_out, grad_out,
    dec_v, enc_v, act_v, gate_v, attr_v, hsend, hout, gin, gnew, agbuf, pbuf, pown, rsx, zsend, zside, rsz, coll,
    load_sem, attr_sem, top_send, top_recv, agz_send, agz_recv, agx_send, agx_recv, rsx_send, rsx_recv,
    rsz_send, rsz_recv, gin_send, gin_recv, coll_send, coll_recv, side_recv, agzs_send, agq_send, rsq_send, zside_send,
):
    feats, width = dec_v.shape[1], dec_v.shape[2]
    tok = top_ref.shape[0]
    rows = nz * tok
    groups = nx
    layer = lax.axis_index("layer")
    feat = lax.axis_index("feat")
    z = feat // nx
    x = feat % nx
    lower = (layer + layers - 1) % layers
    upper = (layer + 1) % layers
    is_top = layer == layers - 1

    def z_peer(d):
        return ((z + d) % nz) * nx + x

    def x_peer(d):
        return z * nx + (x + d) % nx

    def corner(d, e):
        return ((z + d) % nz) * nx + (x + e) % nx

    def cols(j):
        return pl.ds(pl.multiple_of(j * width, 128), width)

    def remote(src, dst, send, recv, where, peer):
        return pltpu.make_async_remote_copy(
            src_ref=src, dst_ref=dst, send_sem=send, recv_sem=recv, device_id=(where, peer), device_id_type=MESH
        )

    def settle(ref, sem):
        pltpu.make_async_copy(ref, ref, sem).wait()

    loads = [pltpu.make_async_copy(act_hbm.at[:, j], act_v.at[j], load_sem.at[2 * nx + j]) for j in range(nx)]
    loads += [pltpu.make_async_copy(dec_hbm.at[:, cols(j)], dec_v.at[j], load_sem.at[j]) for j in range(nx)]
    loads += [pltpu.make_async_copy(enc_hbm.at[:, cols(j)], enc_v.at[j], load_sem.at[nx + j]) for j in range(nx)]
    for load in loads:
        load.start()

    near_z = sorted(range(nz), key=lambda d: min(d, nz - d))
    far_z = [d for d in near_z[::-1] if d]
    sides = side_columns(nz, NEAR_IN)
    backs = side_columns(nz, NEAR_OUT)

    moves = [(0, 0, e) for e in range(1, nx)] + [(0, d, 0) for d in range(1, nz)]
    moves += [(0, d, e) for d in {**sides, **backs} if d for e in (1, -1)]
    moves += [(-1, d, 0) for d in range(nz)] + [(-1, d, e) for d, e in sides.items()]
    moves += [(-a, -b, -c) for a, b, c in moves]
    moves = sorted({(a % layers, b % nz, c % nx) for a, b, c in moves})
    barrier = pltpu.get_barrier_semaphore()
    for a, b, c in moves:
        where = ((layer + a) % layers, ((z + b) % nz) * nx + (x + c) % nx)
        pl.semaphore_signal(barrier, inc=1, device_id=where, device_id_type=MESH)
    pl.semaphore_wait(barrier, len(moves))

    far_x = sorted(range(1, nx), key=lambda d: -min(d, nx - d))
    near_x = far_x[::-1]

    @pl.when(is_top)
    def _():
        pltpu.make_async_copy(top_ref.at[:, cols(x)], hsend.at[x], top_recv).start()
        for d in far_x:
            remote(
                top_ref.at[:, cols((x + d) % nx)], hsend.at[x], top_send, top_recv, layer, x_peer(d)
            ).start()
        settle(hsend, top_recv)

        @pl.loop(0, groups)
        def _(g):
            for d in far_z:
                remote(hsend.at[g], agbuf.at[g, x, z], agz_send, agz_recv.at[g, d], layer, z_peer(d)).start()
            pltpu.make_async_copy(hsend.at[g], agbuf.at[g, x, z], agz_recv.at[g, 0]).start()
            for d, e in sides.items():
                remote(hsend.at[g], agbuf.at[g, x, z], agzs_send, side_recv.at[g, d], layer, corner(d, e)).start()
            gin[g] = hsend[g].astype(jnp.float32)

    tiles = nz * nx
    listed_ids = ids_ref[...]
    width_ids = listed_ids.shape[1]
    eye = lax.broadcasted_iota(jnp.int32, (tiles, tiles), 0) == lax.broadcasted_iota(jnp.int32, (tiles, tiles), 1)
    counts = jnp.sum(jnp.where(eye, jnp.broadcast_to(cnt_ref[...], (tiles, tiles)), 0), axis=1, keepdims=True)
    listed = lax.broadcasted_iota(jnp.int32, (tiles, width_ids), 1) < counts
    blk_dev = feats // BLOCK
    parts = []
    for b in range(blk_dev):
        hit = jnp.where(listed & (listed_ids == feat * blk_dev + b), 1.0, 0.0)
        parts.append(jnp.broadcast_to(jnp.max(hit, axis=1, keepdims=True), (tiles, BLOCK)))
    tile_mask = jnp.concatenate(parts, axis=1).astype(jnp.bfloat16)
    for j in range(nx):
        loads[j].wait()
    row_tile = (lax.broadcasted_iota(jnp.int32, (rows, tiles), 0) // tok) * nx
    col_tile = lax.broadcasted_iota(jnp.int32, (rows, tiles), 1)
    for j in range(groups):
        pick = jnp.where(row_tile + j == col_tile, 1.0, 0.0).astype(jnp.bfloat16)
        mask = jnp.dot(pick, tile_mask, preferred_element_type=jnp.float32)
        gate_v[j] = act_v[j].astype(jnp.float32).reshape(rows, feats) * mask
    for load in loads[nx:]:
        load.wait()

    def pass_on(g, j, k, send, e, d):
        block = agbuf.at[g, j, k]
        remote(block, block, send, agx_recv.at[g, e - 1], layer, x_peer(d)).start()

    def forward(g):
        for d in near_z:
            k = (z + nz - d) % nz
            settle(agbuf.at[g, x, k], agz_recv.at[g, d])
            if d in sides:
                pass_on(g, x, k, agq_send, -sides[d] % nx, -sides[d])
                j = (x + nx - sides[d]) % nx
                settle(agbuf.at[g, j, k], side_recv.at[g, d])
                pass_on(g, j, k, agq_send, 2, sides[d])
            else:
                for e in far_x:
                    pass_on(g, x, k, agx_send, e, e)

    def scores_of(g, j):
        h = agbuf[g, j].reshape(rows, width)
        return lax.dot_general(h, dec_v[j], (((1,), (1,)), ((), ())), preferred_element_type=jnp.float32)

    def out_x(g, d, e):
        k = (z + d) % nz
        remote(
            pbuf.at[g, e - 1, k], rsx.at[g, e - 1, k], rsx_send, rsx_recv.at[g, d], layer, x_peer(e)
        ).start()

    def attribute(g):
        total = scores_of(g, x)
        for d in near_x:
            j = (x + nx - d) % nx
            passed = nz - sum(e % nx == d for e in sides.values())
            settle(agbuf.at[g, j, pl.ds(0, passed)], agx_recv.at[g, d - 1])
            total = total + scores_of(g, j)
        attr = total * gate_v[g]
        attr_v[g] = attr.reshape(nz, tok, feats).astype(jnp.bfloat16)
        attr = attr.astype(jnp.bfloat16)
        pltpu.make_async_copy(attr_v.at[g], attr_out.at[:, g], attr_sem).start()
        plain = [d for d in far_z + [0] if d not in backs]
        for e in far_x:
            part = jnp.dot(attr, enc_v[(x + e) % nx], preferred_element_type=jnp.float32)
            pbuf[g, e - 1] = part.reshape(nz, tok, width).astype(jnp.bfloat16)
            for d in plain[:3]:
                out_x(g, d, e)
        for d in far_z + [0]:
            if d in backs:
                k, e = (z + d) % nz, backs[d]
                remote(pbuf.at[g, 1, k], rsx.at[g, 1, k], rsq_send, rsx_recv.at[g, d], layer, x_peer(-e)).start()
                remote(
                    pbuf.at[g, e % nx - 1, k], rsx.at[g, 0, k], rsq_send, rsx_recv.at[g, d], layer, x_peer(e)
                ).start()
            elif d not in plain[:3]:
                for e in far_x:
                    out_x(g, d, e)
        own = jnp.dot(attr, enc_v[x], preferred_element_type=jnp.float32)
        pown[g] = own.reshape(nz, tok, width)

    def reduce_x(g):
        for d in far_z + [0]:
            k = (z + d) % nz
            total = pown[g, k]
            if d in backs:
                e, i = backs[d], list(backs).index(d)
                settle(rsx.at[g, pl.ds(0, 2), k], rsx_recv.at[g, d])
                total = total + rsx[g, 0, k].astype(jnp.float32)
                other = pbuf[g, -e % nx - 1, k].astype(jnp.float32) + rsx[g, 1, k].astype(jnp.float32)
                zside[g, i] = other.astype(jnp.bfloat16)
                remote(
                    zside.at[g, i], rsz.at[g, nz - 1 + i], zside_send, rsz_recv.at[g], layer, corner(d, -e)
                ).start()
            else:
                settle(rsx.at[g, :, k], rsx_recv.at[g, d])
                for e in near_x:
                    total = total + rsx[g, e - 1, k].astype(jnp.float32)
            zsend[g, k] = total.astype(jnp.bfloat16)
            if d:
                remote(zsend.at[g, k], rsz.at[g, d - 1], rsz_send, rsz_recv.at[g], layer, z_peer(d)).start()

    def reduce_z(g):
        @pl.when(jnp.logical_not(is_top))
        def _():
            settle(gin.at[g], gin_recv.at[g])

        settle(rsz.at[g], rsz_recv.at[g])
        total = zsend[g, z].astype(jnp.float32)
        for d in range(nz - 1 + len(backs)):
            total = total + rsz[g, d].astype(jnp.float32)
        total = total + gin[g]
        gnew[g] = total
        hout[g] = total.astype(jnp.bfloat16)

        @pl.when(layer > 0)
        def _():
            for d in far_z + [0]:
                remote(hout.at[g], agbuf.at[g, x, z], agz_send, agz_recv.at[g, d], lower, z_peer(d)).start()
                if d in sides:
                    where = corner(d, sides[d])
                    remote(hout.at[g], agbuf.at[g, x, z], agzs_send, side_recv.at[g, d], lower, where).start()
            remote(gnew.at[g], gin.at[g], gin_send, gin_recv.at[g], lower, feat).start()

        @pl.when(x != g)
        def _():
            remote(gnew.at[g], coll.at[x], coll_send, coll_recv, layer, z * nx + g).start()

        @pl.when(x == g)
        def _():
            pltpu.make_async_copy(gnew.at[g], coll.at[x], coll_recv).start()

    @pl.loop(0, groups + 1)
    def _(step):
        @pl.when(step < groups)
        def _():
            forward(step)

        @pl.when(step > 0)
        def _():
            reduce_z(step - 1)

        @pl.when(step < groups)
        def _():
            attribute(step)
            reduce_x(step)

    settle(coll, coll_recv)
    for j in range(nx):
        grad_out[:, j * width:(j + 1) * width] = coll[j]

    settle(attr_v, attr_sem)
    for count, sem, small, ref in (
        (len(sides), agx_send, agq_send, agbuf), (len(backs), rsx_send, rsq_send, pbuf)
    ):
        if count < nz:
            settle(ref.at[:, pl.ds(0, nx - 1), pl.ds(0, nz - count)], sem)
        if count:
            settle(ref.at[:, pl.ds(0, 2), pl.ds(0, count)], small)
    if backs:
        settle(zside.at[:, pl.ds(0, len(backs))], zside_send)
    settle(zsend.at[:, pl.ds(0, nz - 1)], rsz_send)
    settle(coll.at[pl.ds(0, nx - 1)], coll_send)

    @pl.when(is_top)
    def _():
        settle(hsend.at[pl.ds(0, nx - 1)], top_send)
        settle(zsend.at[:, pl.ds(0, nz - 1)], agz_send)
        if sides:
            settle(zside.at[:, pl.ds(0, len(sides))], agzs_send)

    @pl.when(layer > 0)
    def _():
        settle(zsend, agz_send)
        if sides:
            settle(zside.at[:, pl.ds(0, len(sides))], agzs_send)
        settle(gnew, gin_send)


def body(nx, top_grad, decoder, encoder, activations, block_ids, block_counts):
    layers = lax.axis_size("layer")
    tiles = lax.axis_size("feat")
    nz = tiles // nx
    dec, enc = decoder[0], encoder[0]
    feats, model = dec.shape
    width = model // nx
    tok = top_grad.shape[0]
    rows = nz * tok
    extra = len(side_columns(nz, NEAR_OUT))
    slots = max(1, extra, len(side_columns(nz, NEAR_IN)))
    act = activations[0].reshape(nz, nx, tok, feats)
    bf16, f32 = jnp.bfloat16, jnp.float32
    dma = pltpu.SemaphoreType.DMA
    vmem = pl.BlockSpec(memory_space=pltpu.VMEM)
    hbm = pl.BlockSpec(memory_space=pl.ANY)
    attr, grads = pl.pallas_call(
        functools.partial(kernel, layers, nz, nx),
        out_shape=(
            jax.ShapeDtypeStruct((nz, nx, tok, feats), bf16),
            jax.ShapeDtypeStruct((tok, model), f32),
        ),
        in_specs=[vmem, hbm, hbm, hbm, vmem, vmem],
        out_specs=(hbm, vmem),
        scratch_shapes=[
            pltpu.VMEM((nx, feats, width), bf16),
            pltpu.VMEM((nx, feats, width), bf16),
            pltpu.VMEM((nx, nz, tok, feats), bf16),
            pltpu.VMEM((nx, rows, feats), f32),
            pltpu.VMEM((nx, nz, tok, feats), bf16),
            pltpu.VMEM((nx, tok, width), bf16),
            pltpu.VMEM((nx, tok, width), bf16),
            pltpu.VMEM((nx, tok, width), f32),
            pltpu.VMEM((nx, tok, width), f32),
            pltpu.VMEM((nx, nx, nz, tok, width), bf16),
            pltpu.VMEM((nx, nx - 1, nz, tok, width), bf16),
            pltpu.VMEM((nx, nz, tok, width), f32),
            pltpu.VMEM((nx, nx - 1, nz, tok, width), bf16),
            pltpu.VMEM((nx, nz, tok, width), bf16),
            pltpu.VMEM((nx, slots, tok, width), bf16),
            pltpu.VMEM((nx, nz - 1 + extra, tok, width), bf16),
            pltpu.VMEM((nx, tok, width), f32),
            dma((3 * nx,)),
            dma,
            dma,
            dma,
            dma,
            dma((nx, nz)),
            dma,
            dma((nx, nx - 1)),
            dma,
            dma((nx, nz)),
            dma,
            dma((nx,)),
            dma,
            dma((nx,)),
            dma,
            dma,
            dma((nx, nz)),
            dma,
            dma,
            dma,
            dma,
        ],
        compiler_params=pltpu.CompilerParams(
            collective_id=0, has_side_effects=True, vmem_limit_bytes=60 * 1024 * 1024
        ),
    )(top_grad, dec, enc, act, block_ids[0], block_counts)
    return (attr.reshape(1, tiles * tok, feats), grads[None])


def solution(mesh, nx=NX):
    placed = (
        P("feat", None),
        P("layer", "feat", None),
        P("layer", "feat", None),
        P("layer", None, "feat"),
        P("layer", None, None),
        P("layer", None),
    )
    return jax.shard_map(
        functools.partial(body, nx),
        mesh=mesh,
        in_specs=placed,
        out_specs=(P("layer", None, "feat"), P("layer", "feat", None)),
        check_vma=False,
    )
```

```python
import functools

import jax
import jax.numpy as jnp
from jax import lax
from jax.experimental import pallas as pl
from jax.experimental.pallas import tpu as pltpu
from jax.sharding import PartitionSpec as P

BLOCK = 128
MESH = pl.DeviceIdType.MESH
NX = 4
NEAR_IN = 2
NEAR_OUT = 2


def side_columns(nz, reach):
    near = [d for d in sorted(range(nz), key=lambda d: min(d, nz - d)) if min(d, nz - d) <= reach]
    return {d: 1 - 2 * (i % 2) for i, d in enumerate(near)}


def kernel(
    layers, nz, nx, top_ref, dec_hbm, enc_hbm, act_hbm, ids_ref, cnt_ref, attr_out, grad_out,
    dec_v, enc_v, act_v, gate_v, attr_v, hsend, hout, gin, gnew, agbuf, pbuf, pown, rsx, zsend, zside, rsz, coll,
    load_sem, attr_sem, top_send, top_recv, agz_send, agz_recv, agx_send, agx_recv, rsx_send, rsx_recv,
    rsz_send, rsz_recv, gin_send, gin_recv, coll_send, coll_recv, side_recv, agzs_send, agq_send, rsq_send, zside_send,
):
    feats, width = dec_v.shape[1], dec_v.shape[2]
    tok = top_ref.shape[0]
    rows = nz * tok
    groups = nx
    layer = lax.axis_index("layer")
    feat = lax.axis_index("feat")
    z = feat // nx
    x = feat % nx
    lower = (layer + layers - 1) % layers
    upper = (layer + 1) % layers
    is_top = layer == layers - 1

    def z_peer(d):
        return ((z + d) % nz) * nx + x

    def x_peer(d):
        return z * nx + (x + d) % nx

    def corner(d, e):
        return ((z + d) % nz) * nx + (x + e) % nx

    def cols(j):
        return pl.ds(pl.multiple_of(j * width, 128), width)

    def remote(src, dst, send, recv, where, peer):
        return pltpu.make_async_remote_copy(
            src_ref=src, dst_ref=dst, send_sem=send, recv_sem=recv, device_id=(where, peer), device_id_type=MESH
        )

    def settle(ref, sem):
        pltpu.make_async_copy(ref, ref, sem).wait()

    loads = [pltpu.make_async_copy(act_hbm.at[:, j], act_v.at[j], load_sem.at[2 * nx + j]) for j in range(nx)]
    loads += [pltpu.make_async_copy(dec_hbm.at[:, cols(j)], dec_v.at[j], load_sem.at[j]) for j in range(nx)]
    loads += [pltpu.make_async_copy(enc_hbm.at[:, cols(j)], enc_v.at[j], load_sem.at[nx + j]) for j in range(nx)]
    for load in loads:
        load.start()

    near_z = sorted(range(nz), key=lambda d: min(d, nz - d))
    far_z = [d for d in near_z[::-1] if d]
    sides = side_columns(nz, NEAR_IN)
    backs = side_columns(nz, NEAR_OUT)

    moves = [(0, 0, e) for e in range(1, nx)] + [(0, d, 0) for d in range(1, nz)]
    moves += [(0, d, e) for d in {**sides, **backs} if d for e in (1, -1)]
    moves += [(-1, d, 0) for d in range(nz)] + [(-1, d, e) for d, e in sides.items()]
    moves += [(-a, -b, -c) for a, b, c in moves]
    moves = sorted({(a % layers, b % nz, c % nx) for a, b, c in moves})
    barrier = pltpu.get_barrier_semaphore()
    for a, b, c in moves:
        where = ((layer + a) % layers, ((z + b) % nz) * nx + (x + c) % nx)
        pl.semaphore_signal(barrier, inc=1, device_id=where, device_id_type=MESH)
    pl.semaphore_wait(barrier, len(moves))

    far_x = sorted(range(1, nx), key=lambda d: -min(d, nx - d))
    near_x = far_x[::-1]

    @pl.when(is_top)
    def _():
        pltpu.make_async_copy(top_ref.at[:, cols(x)], hsend.at[x], top_recv).start()
        for d in far_x:
            remote(
                top_ref.at[:, cols((x + d) % nx)], hsend.at[x], top_send, top_recv, layer, x_peer(d)
            ).start()
        settle(hsend, top_recv)

        @pl.loop(0, groups)
        def _(g):
            for d in far_z:
                remote(hsend.at[g], agbuf.at[g, x, z], agz_send, agz_recv.at[g, d], layer, z_peer(d)).start()
            pltpu.make_async_copy(hsend.at[g], agbuf.at[g, x, z], agz_recv.at[g, 0]).start()
            for d, e in sides.items():
                remote(hsend.at[g], agbuf.at[g, x, z], agzs_send, side_recv.at[g, d], layer, corner(d, e)).start()
            gin[g] = hsend[g].astype(jnp.float32)

    tiles = nz * nx
    listed_ids = ids_ref[...]
    width_ids = listed_ids.shape[1]
    eye = lax.broadcasted_iota(jnp.int32, (tiles, tiles), 0) == lax.broadcasted_iota(jnp.int32, (tiles, tiles), 1)
    counts = jnp.sum(jnp.where(eye, jnp.broadcast_to(cnt_ref[...], (tiles, tiles)), 0), axis=1, keepdims=True)
    listed = lax.broadcasted_iota(jnp.int32, (tiles, width_ids), 1) < counts
    blk_dev = feats // BLOCK
    parts = []
    for b in range(blk_dev):
        hit = jnp.where(listed & (listed_ids == feat * blk_dev + b), 1.0, 0.0)
        parts.append(jnp.broadcast_to(jnp.max(hit, axis=1, keepdims=True), (tiles, BLOCK)))
    tile_mask = jnp.concatenate(parts, axis=1).astype(jnp.bfloat16)
    for j in range(nx):
        loads[j].wait()
    row_tile = (lax.broadcasted_iota(jnp.int32, (rows, tiles), 0) // tok) * nx
    col_tile = lax.broadcasted_iota(jnp.int32, (rows, tiles), 1)
    for j in range(groups):
        pick = jnp.where(row_tile + j == col_tile, 1.0, 0.0).astype(jnp.bfloat16)
        mask = jnp.dot(pick, tile_mask, preferred_element_type=jnp.float32)
        gate_v[j] = act_v[j].astype(jnp.float32).reshape(rows, feats) * mask
    for load in loads[nx:]:
        load.wait()

    def pass_on(g, j, k, send, e, d):
        block = agbuf.at[g, j, k]
        remote(block, block, send, agx_recv.at[g, e - 1], layer, x_peer(d)).start()

    arrivals = [(min(d, nz - d), 0, d) for d in near_z] + [(min(d, nz - d) + 1, 1, d) for d in sides]

    def forward(g):
        for hops, second, d in sorted(arrivals):
            k = (z + nz - d) % nz
            if second:
                j = (x + nx - sides[d]) % nx
                settle(agbuf.at[g, j, k], side_recv.at[g, d])
                pass_on(g, j, k, agq_send, 2, sides[d])
                continue
            settle(agbuf.at[g, x, k], agz_recv.at[g, d])
            if d in sides:
                pass_on(g, x, k, agq_send, -sides[d] % nx, -sides[d])
            else:
                for e in far_x:
                    pass_on(g, x, k, agx_send, e, e)

    def scores_of(g, j):
        h = agbuf[g, j].reshape(rows, width)
        return lax.dot_general(h, dec_v[j], (((1,), (1,)), ((), ())), preferred_element_type=jnp.float32)

    def out_x(g, d, e):
        k = (z + d) % nz
        remote(
            pbuf.at[g, e - 1, k], rsx.at[g, e - 1, k], rsx_send, rsx_recv.at[g, d], layer, x_peer(e)
        ).start()

    def attribute(g):
        total = scores_of(g, x)
        for d in near_x:
            j = (x + nx - d) % nx
            passed = nz - sum(e % nx == d for e in sides.values())
            settle(agbuf.at[g, j, pl.ds(0, passed)], agx_recv.at[g, d - 1])
            total = total + scores_of(g, j)
        attr = total * gate_v[g]
        attr_v[g] = attr.reshape(nz, tok, feats).astype(jnp.bfloat16)
        attr = attr.astype(jnp.bfloat16)
        pltpu.make_async_copy(attr_v.at[g], attr_out.at[:, g], attr_sem).start()
        plain = [d for d in far_z + [0] if d not in backs]
        for e in far_x:
            part = jnp.dot(attr, enc_v[(x + e) % nx], preferred_element_type=jnp.float32)
            pbuf[g, e - 1] = part.reshape(nz, tok, width).astype(jnp.bfloat16)
            for d in plain[:3]:
                out_x(g, d, e)
        for d in far_z + [0]:
            if d in backs:
                k, e = (z + d) % nz, backs[d]
                remote(pbuf.at[g, 1, k], rsx.at[g, 1, k], rsq_send, rsx_recv.at[g, d], layer, x_peer(-e)).start()
                remote(
                    pbuf.at[g, e % nx - 1, k], rsx.at[g, 0, k], rsq_send, rsx_recv.at[g, d], layer, x_peer(e)
                ).start()
            elif d not in plain[:3]:
                for e in far_x:
                    out_x(g, d, e)
        own = jnp.dot(attr, enc_v[x], preferred_element_type=jnp.float32)
        pown[g] = own.reshape(nz, tok, width)

    def reduce_x(g):
        for d in far_z + [0]:
            k = (z + d) % nz
            total = pown[g, k]
            if d in backs:
                e, i = backs[d], list(backs).index(d)
                settle(rsx.at[g, pl.ds(0, 2), k], rsx_recv.at[g, d])
                total = total + rsx[g, 0, k].astype(jnp.float32)
                other = pbuf[g, -e % nx - 1, k].astype(jnp.float32) + rsx[g, 1, k].astype(jnp.float32)
                zside[g, i] = other.astype(jnp.bfloat16)
                remote(
                    zside.at[g, i], rsz.at[g, nz - 1 + i], zside_send, rsz_recv.at[g], layer, corner(d, -e)
                ).start()
            else:
                settle(rsx.at[g, :, k], rsx_recv.at[g, d])
                for e in near_x:
                    total = total + rsx[g, e - 1, k].astype(jnp.float32)
            zsend[g, k] = total.astype(jnp.bfloat16)
            if d:
                remote(zsend.at[g, k], rsz.at[g, d - 1], rsz_send, rsz_recv.at[g], layer, z_peer(d)).start()

    def reduce_z(g):
        @pl.when(jnp.logical_not(is_top))
        def _():
            settle(gin.at[g], gin_recv.at[g])

        settle(rsz.at[g], rsz_recv.at[g])
        total = zsend[g, z].astype(jnp.float32)
        for d in range(nz - 1 + len(backs)):
            total = total + rsz[g, d].astype(jnp.float32)
        total = total + gin[g]
        gnew[g] = total
        hout[g] = total.astype(jnp.bfloat16)

        @pl.when(layer > 0)
        def _():
            for d in far_z + [0]:
                remote(hout.at[g], agbuf.at[g, x, z], agz_send, agz_recv.at[g, d], lower, z_peer(d)).start()
                if d in sides:
                    where = corner(d, sides[d])
                    remote(hout.at[g], agbuf.at[g, x, z], agzs_send, side_recv.at[g, d], lower, where).start()
            remote(gnew.at[g], gin.at[g], gin_send, gin_recv.at[g], lower, feat).start()

        @pl.when(x != g)
        def _():
            remote(gnew.at[g], coll.at[x], coll_send, coll_recv, layer, z * nx + g).start()

        @pl.when(x == g)
        def _():
            pltpu.make_async_copy(gnew.at[g], coll.at[x], coll_recv).start()

    @pl.loop(0, groups + 1)
    def _(step):
        @pl.when(step < groups)
        def _():
            forward(step)

        @pl.when(step > 0)
        def _():
            reduce_z(step - 1)

        @pl.when(step < groups)
        def _():
            attribute(step)
            reduce_x(step)

    settle(coll, coll_recv)
    for j in range(nx):
        grad_out[:, j * width:(j + 1) * width] = coll[j]

    settle(attr_v, attr_sem)
    for count, sem, small, ref in (
        (len(sides), agx_send, agq_send, agbuf), (len(backs), rsx_send, rsq_send, pbuf)
    ):
        if count < nz:
            settle(ref.at[:, pl.ds(0, nx - 1), pl.ds(0, nz - count)], sem)
        if count:
            settle(ref.at[:, pl.ds(0, 2), pl.ds(0, count)], small)
    if backs:
        settle(zside.at[:, pl.ds(0, len(backs))], zside_send)
    settle(zsend.at[:, pl.ds(0, nz - 1)], rsz_send)
    settle(coll.at[pl.ds(0, nx - 1)], coll_send)

    @pl.when(is_top)
    def _():
        settle(hsend.at[pl.ds(0, nx - 1)], top_send)
        settle(zsend.at[:, pl.ds(0, nz - 1)], agz_send)
        if sides:
            settle(zside.at[:, pl.ds(0, len(sides))], agzs_send)

    @pl.when(layer > 0)
    def _():
        settle(zsend, agz_send)
        if sides:
            settle(zside.at[:, pl.ds(0, len(sides))], agzs_send)
        settle(gnew, gin_send)


def hand_over(attr_ref, grad_ref, attr_out, grad_out):
    attr_out[...] = attr_ref[...]
    grad_out[...] = grad_ref[...]


def body(nx, top_grad, decoder, encoder, activations, block_ids, block_counts):
    layers = lax.axis_size("layer")
    tiles = lax.axis_size("feat")
    nz = tiles // nx
    dec, enc = decoder[0], encoder[0]
    feats, model = dec.shape
    width = model // nx
    tok = top_grad.shape[0]
    rows = nz * tok
    extra = len(side_columns(nz, NEAR_OUT))
    slots = max(1, extra, len(side_columns(nz, NEAR_IN)))
    act = activations[0].reshape(nz, nx, tok, feats)
    bf16, f32 = jnp.bfloat16, jnp.float32
    dma = pltpu.SemaphoreType.DMA
    vmem = pl.BlockSpec(memory_space=pltpu.VMEM)
    hbm = pl.BlockSpec(memory_space=pl.ANY)
    attr, grads = pl.pallas_call(
        functools.partial(kernel, layers, nz, nx),
        out_shape=(
            jax.ShapeDtypeStruct((nz, nx, tok, feats), bf16),
            jax.ShapeDtypeStruct((tok, model), f32),
        ),
        in_specs=[vmem, hbm, hbm, hbm, vmem, vmem],
        out_specs=(hbm, vmem),
        scratch_shapes=[
            pltpu.VMEM((nx, feats, width), bf16),
            pltpu.VMEM((nx, feats, width), bf16),
            pltpu.VMEM((nx, nz, tok, feats), bf16),
            pltpu.VMEM((nx, rows, feats), f32),
            pltpu.VMEM((nx, nz, tok, feats), bf16),
            pltpu.VMEM((nx, tok, width), bf16),
            pltpu.VMEM((nx, tok, width), bf16),
            pltpu.VMEM((nx, tok, width), f32),
            pltpu.VMEM((nx, tok, width), f32),
            pltpu.VMEM((nx, nx, nz, tok, width), bf16),
            pltpu.VMEM((nx, nx - 1, nz, tok, width), bf16),
            pltpu.VMEM((nx, nz, tok, width), f32),
            pltpu.VMEM((nx, nx - 1, nz, tok, width), bf16),
            pltpu.VMEM((nx, nz, tok, width), bf16),
            pltpu.VMEM((nx, slots, tok, width), bf16),
            pltpu.VMEM((nx, nz - 1 + extra, tok, width), bf16),
            pltpu.VMEM((nx, tok, width), f32),
            dma((3 * nx,)),
            dma,
            dma,
            dma,
            dma,
            dma((nx, nz)),
            dma,
            dma((nx, nx - 1)),
            dma,
            dma((nx, nz)),
            dma,
            dma((nx,)),
            dma,
            dma((nx,)),
            dma,
            dma,
            dma((nx, nz)),
            dma,
            dma,
            dma,
            dma,
        ],
        compiler_params=pltpu.CompilerParams(
            collective_id=0, has_side_effects=True, vmem_limit_bytes=60 * 1024 * 1024
        ),
    )(top_grad, dec, enc, act, block_ids[0], block_counts)
    attr, grads = pl.pallas_call(
        hand_over,
        out_shape=(
            jax.ShapeDtypeStruct((nz, nx, tok, feats), bf16),
            jax.ShapeDtypeStruct((tok, model), f32),
        ),
        in_specs=[vmem, vmem],
        out_specs=(vmem, vmem),
    )(attr, grads)
    return (attr.reshape(1, tiles * tok, feats), grads[None])


def solution(mesh, nx=NX):
    placed = (
        P("feat", None),
        P("layer", "feat", None),
        P("layer", "feat", None),
        P("layer", None, "feat"),
        P("layer", None, None),
        P("layer", None),
    )
    return jax.shard_map(
        functools.partial(body, nx),
        mesh=mesh,
        in_specs=placed,
        out_specs=(P("layer", None, "feat"), P("layer", "feat", None)),
        check_vma=False,
    )
```

```python
import functools

import jax
import jax.numpy as jnp
from jax import lax
from jax.experimental import pallas as pl
from jax.experimental.pallas import tpu as pltpu
from jax.sharding import PartitionSpec as P

BLOCK = 128
MESH = pl.DeviceIdType.MESH
NX = 4
NEAR_IN = 2
NEAR_OUT = 2


def side_columns(nz, reach):
    near = [d for d in sorted(range(nz), key=lambda d: min(d, nz - d)) if min(d, nz - d) <= reach]
    return {d: 1 - 2 * (i % 2) for i, d in enumerate(near)}


def kernel(
    layers, nz, nx, top_ref, dec_hbm, enc_hbm, act_hbm, ids_ref, cnt_ref, attr_out, grad_out,
    dec_v, enc_v, act_v, gate_v, attr_v, hsend, hout, gin, gnew, agbuf, pbuf, pown, rsx, zsend, zside, rsz, coll, begun,
    load_sem, attr_sem, top_send, top_recv, agz_send, agz_recv, agx_send, agx_recv, rsx_send, rsx_recv,
    rsz_send, rsz_recv, gin_send, gin_recv, coll_send, coll_recv, side_recv, agzs_send, agq_send, rsq_send, zside_send,
):
    feats, width = dec_v.shape[1], dec_v.shape[2]
    tok = top_ref.shape[0]
    rows = nz * tok
    groups = nx
    layer = lax.axis_index("layer")
    feat = lax.axis_index("feat")
    z = feat // nx
    x = feat % nx
    lower = (layer + layers - 1) % layers
    upper = (layer + 1) % layers
    is_top = layer == layers - 1

    def z_peer(d):
        return ((z + d) % nz) * nx + x

    def x_peer(d):
        return z * nx + (x + d) % nx

    def corner(d, e):
        return ((z + d) % nz) * nx + (x + e) % nx

    def cols(j):
        return pl.ds(pl.multiple_of(j * width, 128), width)

    def remote(src, dst, send, recv, where, peer):
        return pltpu.make_async_remote_copy(
            src_ref=src, dst_ref=dst, send_sem=send, recv_sem=recv, device_id=(where, peer), device_id_type=MESH
        )

    def settle(ref, sem):
        pltpu.make_async_copy(ref, ref, sem).wait()

    loads = [pltpu.make_async_copy(act_hbm.at[:, j], act_v.at[j], load_sem.at[2 * nx + j]) for j in range(nx)]
    loads += [pltpu.make_async_copy(dec_hbm.at[:, cols(j)], dec_v.at[j], load_sem.at[j]) for j in range(nx)]
    loads += [pltpu.make_async_copy(enc_hbm.at[:, cols(j)], enc_v.at[j], load_sem.at[nx + j]) for j in range(nx)]
    for load in loads:
        load.start()

    near_z = sorted(range(nz), key=lambda d: min(d, nz - d))
    far_z = [d for d in near_z[::-1] if d]
    sides = side_columns(nz, NEAR_IN)
    backs = side_columns(nz, NEAR_OUT)

    moves = [(0, 0, e) for e in range(1, nx)] + [(0, d, 0) for d in range(1, nz)]
    moves += [(0, d, e) for d in {**sides, **backs} if d for e in (1, -1)]
    moves += [(-1, d, 0) for d in range(nz)] + [(-1, d, e) for d, e in sides.items()]
    moves += [(-a, -b, -c) for a, b, c in moves]
    moves = sorted({(a % layers, b % nz, c % nx) for a, b, c in moves})
    barrier = pltpu.get_barrier_semaphore()
    for a, b, c in moves:
        where = ((layer + a) % layers, ((z + b) % nz) * nx + (x + c) % nx)
        pl.semaphore_signal(barrier, inc=1, device_id=where, device_id_type=MESH)
    pl.semaphore_wait(barrier, len(moves))

    far_x = sorted(range(1, nx), key=lambda d: -min(d, nx - d))
    near_x = far_x[::-1]

    @pl.when(is_top)
    def _():
        pltpu.make_async_copy(top_ref.at[:, cols(x)], hsend.at[x], top_recv).start()
        for d in far_x:
            remote(
                top_ref.at[:, cols((x + d) % nx)], hsend.at[x], top_send, top_recv, layer, x_peer(d)
            ).start()
        settle(hsend, top_recv)

        @pl.loop(0, groups)
        def _(g):
            for d in far_z:
                remote(hsend.at[g], agbuf.at[g, x, z], agz_send, agz_recv.at[g, d], layer, z_peer(d)).start()
            pltpu.make_async_copy(hsend.at[g], agbuf.at[g, x, z], agz_recv.at[g, 0]).start()
            for d, e in sides.items():
                remote(hsend.at[g], agbuf.at[g, x, z], agzs_send, side_recv.at[g, d], layer, corner(d, e)).start()
            gin[g] = hsend[g].astype(jnp.float32)

    tiles = nz * nx
    listed_ids = ids_ref[...]
    width_ids = listed_ids.shape[1]
    eye = lax.broadcasted_iota(jnp.int32, (tiles, tiles), 0) == lax.broadcasted_iota(jnp.int32, (tiles, tiles), 1)
    counts = jnp.sum(jnp.where(eye, jnp.broadcast_to(cnt_ref[...], (tiles, tiles)), 0), axis=1, keepdims=True)
    listed = lax.broadcasted_iota(jnp.int32, (tiles, width_ids), 1) < counts
    blk_dev = feats // BLOCK
    parts = []
    for b in range(blk_dev):
        hit = jnp.where(listed & (listed_ids == feat * blk_dev + b), 1.0, 0.0)
        parts.append(jnp.broadcast_to(jnp.max(hit, axis=1, keepdims=True), (tiles, BLOCK)))
    tile_mask = jnp.concatenate(parts, axis=1).astype(jnp.bfloat16)
    for j in range(nx):
        loads[j].wait()
    row_tile = (lax.broadcasted_iota(jnp.int32, (rows, tiles), 0) // tok) * nx
    col_tile = lax.broadcasted_iota(jnp.int32, (rows, tiles), 1)
    for j in range(groups):
        pick = jnp.where(row_tile + j == col_tile, 1.0, 0.0).astype(jnp.bfloat16)
        mask = jnp.dot(pick, tile_mask, preferred_element_type=jnp.float32)
        gate_v[j] = act_v[j].astype(jnp.float32).reshape(rows, feats) * mask
    for load in loads[nx:]:
        load.wait()

    def pass_on(g, j, k, send, e, d):
        block = agbuf.at[g, j, k]
        remote(block, block, send, agx_recv.at[g, e - 1], layer, x_peer(d)).start()

    arrivals = [(min(d, nz - d), 0, d) for d in near_z] + [(min(d, nz - d) + 1, 1, d) for d in sides]

    def forward(g):
        for hops, second, d in sorted(arrivals):
            k = (z + nz - d) % nz
            if second:
                j = (x + nx - sides[d]) % nx
                settle(agbuf.at[g, j, k], side_recv.at[g, d])
                pass_on(g, j, k, agq_send, 2, sides[d])
                continue
            settle(agbuf.at[g, x, k], agz_recv.at[g, d])
            if d in sides:
                pass_on(g, x, k, agq_send, -sides[d] % nx, -sides[d])
            else:
                for e in far_x:
                    pass_on(g, x, k, agx_send, e, e)

    def scores_of(g, j):
        h = agbuf[g, j].reshape(rows, width)
        return lax.dot_general(h, dec_v[j], (((1,), (1,)), ((), ())), preferred_element_type=jnp.float32)

    def out_x(g, d, e):
        k = (z + d) % nz
        remote(
            pbuf.at[g, e - 1, k], rsx.at[g, e - 1, k], rsx_send, rsx_recv.at[g, d], layer, x_peer(e)
        ).start()

    def attribute(g):
        total = begun[...]
        for d in near_x:
            j = (x + nx - d) % nx
            passed = nz - sum(e % nx == d for e in sides.values())
            settle(agbuf.at[g, j, pl.ds(0, passed)], agx_recv.at[g, d - 1])
            total = total + scores_of(g, j)
        attr = total * gate_v[g]
        attr_v[g] = attr.reshape(nz, tok, feats).astype(jnp.bfloat16)
        attr = attr.astype(jnp.bfloat16)
        pltpu.make_async_copy(attr_v.at[g], attr_out.at[:, g], attr_sem).start()
        plain = [d for d in far_z + [0] if d not in backs]
        for e in far_x:
            part = jnp.dot(attr, enc_v[(x + e) % nx], preferred_element_type=jnp.float32)
            pbuf[g, e - 1] = part.reshape(nz, tok, width).astype(jnp.bfloat16)
            for d in plain[:3]:
                out_x(g, d, e)
        for d in far_z + [0]:
            if d in backs:
                k, e = (z + d) % nz, backs[d]
                remote(pbuf.at[g, 1, k], rsx.at[g, 1, k], rsq_send, rsx_recv.at[g, d], layer, x_peer(-e)).start()
                remote(
                    pbuf.at[g, e % nx - 1, k], rsx.at[g, 0, k], rsq_send, rsx_recv.at[g, d], layer, x_peer(e)
                ).start()
            elif d not in plain[:3]:
                for e in far_x:
                    out_x(g, d, e)
        own = jnp.dot(attr, enc_v[x], preferred_element_type=jnp.float32)
        pown[g] = own.reshape(nz, tok, width)

    def reduce_x(g):
        for d in far_z + [0]:
            k = (z + d) % nz
            total = pown[g, k]
            if d in backs:
                e, i = backs[d], list(backs).index(d)
                settle(rsx.at[g, pl.ds(0, 2), k], rsx_recv.at[g, d])
                total = total + rsx[g, 0, k].astype(jnp.float32)
                other = pbuf[g, -e % nx - 1, k].astype(jnp.float32) + rsx[g, 1, k].astype(jnp.float32)
                zside[g, i] = other.astype(jnp.bfloat16)
                remote(
                    zside.at[g, i], rsz.at[g, nz - 1 + i], zside_send, rsz_recv.at[g], layer, corner(d, -e)
                ).start()
            else:
                settle(rsx.at[g, :, k], rsx_recv.at[g, d])
                for e in near_x:
                    total = total + rsx[g, e - 1, k].astype(jnp.float32)
            zsend[g, k] = total.astype(jnp.bfloat16)
            if d:
                remote(zsend.at[g, k], rsz.at[g, d - 1], rsz_send, rsz_recv.at[g], layer, z_peer(d)).start()

    def reduce_z(g):
        @pl.when(jnp.logical_not(is_top))
        def _():
            settle(gin.at[g], gin_recv.at[g])

        settle(rsz.at[g], rsz_recv.at[g])
        total = zsend[g, z].astype(jnp.float32)
        for d in range(nz - 1 + len(backs)):
            total = total + rsz[g, d].astype(jnp.float32)
        total = total + gin[g]
        gnew[g] = total
        hout[g] = total.astype(jnp.bfloat16)

        @pl.when(layer > 0)
        def _():
            for d in far_z + [0]:
                remote(hout.at[g], agbuf.at[g, x, z], agz_send, agz_recv.at[g, d], lower, z_peer(d)).start()
                if d in sides:
                    where = corner(d, sides[d])
                    remote(hout.at[g], agbuf.at[g, x, z], agzs_send, side_recv.at[g, d], lower, where).start()
            remote(gnew.at[g], gin.at[g], gin_send, gin_recv.at[g], lower, feat).start()

        @pl.when(x != g)
        def _():
            remote(gnew.at[g], coll.at[x], coll_send, coll_recv, layer, z * nx + g).start()

        @pl.when(x == g)
        def _():
            pltpu.make_async_copy(gnew.at[g], coll.at[x], coll_recv).start()

    @pl.loop(0, groups + 1)
    def _(step):
        @pl.when(step < groups)
        def _():
            forward(step)
            begun[...] = scores_of(step, x)

        @pl.when(step > 0)
        def _():
            reduce_z(step - 1)

        @pl.when(step < groups)
        def _():
            attribute(step)
            reduce_x(step)

    settle(coll, coll_recv)
    for j in range(nx):
        grad_out[:, j * width:(j + 1) * width] = coll[j]

    settle(attr_v, attr_sem)
    for count, sem, small, ref in (
        (len(sides), agx_send, agq_send, agbuf), (len(backs), rsx_send, rsq_send, pbuf)
    ):
        if count < nz:
            settle(ref.at[:, pl.ds(0, nx - 1), pl.ds(0, nz - count)], sem)
        if count:
            settle(ref.at[:, pl.ds(0, 2), pl.ds(0, count)], small)
    if backs:
        settle(zside.at[:, pl.ds(0, len(backs))], zside_send)
    settle(zsend.at[:, pl.ds(0, nz - 1)], rsz_send)
    settle(coll.at[pl.ds(0, nx - 1)], coll_send)

    @pl.when(is_top)
    def _():
        settle(hsend.at[pl.ds(0, nx - 1)], top_send)
        settle(zsend.at[:, pl.ds(0, nz - 1)], agz_send)
        if sides:
            settle(zside.at[:, pl.ds(0, len(sides))], agzs_send)

    @pl.when(layer > 0)
    def _():
        settle(zsend, agz_send)
        if sides:
            settle(zside.at[:, pl.ds(0, len(sides))], agzs_send)
        settle(gnew, gin_send)


def hand_over(attr_ref, grad_ref, attr_out, grad_out):
    attr_out[...] = attr_ref[...]
    grad_out[...] = grad_ref[...]


def body(nx, top_grad, decoder, encoder, activations, block_ids, block_counts):
    layers = lax.axis_size("layer")
    tiles = lax.axis_size("feat")
    nz = tiles // nx
    dec, enc = decoder[0], encoder[0]
    feats, model = dec.shape
    width = model // nx
    tok = top_grad.shape[0]
    rows = nz * tok
    extra = len(side_columns(nz, NEAR_OUT))
    slots = max(1, extra, len(side_columns(nz, NEAR_IN)))
    act = activations[0].reshape(nz, nx, tok, feats)
    bf16, f32 = jnp.bfloat16, jnp.float32
    dma = pltpu.SemaphoreType.DMA
    vmem = pl.BlockSpec(memory_space=pltpu.VMEM)
    hbm = pl.BlockSpec(memory_space=pl.ANY)
    attr, grads = pl.pallas_call(
        functools.partial(kernel, layers, nz, nx),
        out_shape=(
            jax.ShapeDtypeStruct((nz, nx, tok, feats), bf16),
            jax.ShapeDtypeStruct((tok, model), f32),
        ),
        in_specs=[vmem, hbm, hbm, hbm, vmem, vmem],
        out_specs=(hbm, vmem),
        scratch_shapes=[
            pltpu.VMEM((nx, feats, width), bf16),
            pltpu.VMEM((nx, feats, width), bf16),
            pltpu.VMEM((nx, nz, tok, feats), bf16),
            pltpu.VMEM((nx, rows, feats), f32),
            pltpu.VMEM((nx, nz, tok, feats), bf16),
            pltpu.VMEM((nx, tok, width), bf16),
            pltpu.VMEM((nx, tok, width), bf16),
            pltpu.VMEM((nx, tok, width), f32),
            pltpu.VMEM((nx, tok, width), f32),
            pltpu.VMEM((nx, nx, nz, tok, width), bf16),
            pltpu.VMEM((nx, nx - 1, nz, tok, width), bf16),
            pltpu.VMEM((nx, nz, tok, width), f32),
            pltpu.VMEM((nx, nx - 1, nz, tok, width), bf16),
            pltpu.VMEM((nx, nz, tok, width), bf16),
            pltpu.VMEM((nx, slots, tok, width), bf16),
            pltpu.VMEM((nx, nz - 1 + extra, tok, width), bf16),
            pltpu.VMEM((nx, tok, width), f32),
            pltpu.VMEM((rows, feats), f32),
            dma((3 * nx,)),
            dma,
            dma,
            dma,
            dma,
            dma((nx, nz)),
            dma,
            dma((nx, nx - 1)),
            dma,
            dma((nx, nz)),
            dma,
            dma((nx,)),
            dma,
            dma((nx,)),
            dma,
            dma,
            dma((nx, nz)),
            dma,
            dma,
            dma,
            dma,
        ],
        compiler_params=pltpu.CompilerParams(
            collective_id=0, has_side_effects=True, vmem_limit_bytes=60 * 1024 * 1024
        ),
    )(top_grad, dec, enc, act, block_ids[0], block_counts)
    attr, grads = pl.pallas_call(
        hand_over,
        out_shape=(
            jax.ShapeDtypeStruct((nz, nx, tok, feats), bf16),
            jax.ShapeDtypeStruct((tok, model), f32),
        ),
        in_specs=[vmem, vmem],
        out_specs=(vmem, vmem),
    )(attr, grads)
    return (attr.reshape(1, tiles * tok, feats), grads[None])


def solution(mesh, nx=NX):
    placed = (
        P("feat", None),
        P("layer", "feat", None),
        P("layer", "feat", None),
        P("layer", None, "feat"),
        P("layer", None, None),
        P("layer", None),
    )
    return jax.shard_map(
        functools.partial(body, nx),
        mesh=mesh,
        in_specs=placed,
        out_specs=(P("layer", None, "feat"), P("layer", "feat", None)),
        check_vma=False,
    )
```
